512 devices in a mesh: tm: 64 (over y_lo, z, core), user: 8 (over x, y_hi).
Axes of the slice: x: 4, y: 8 (y_hi: 2, y_lo: 4; y = y_hi * 4 + y_lo), z: 8, core: 2. Of those that a mesh axis runs over, the one named last changes fastest.
Arguments:
- events: bfloat16 [256, 4096, 256], P('user', 'tm'), parts along dimension 0, may hold values from -6 to 6
- lengths: int32 [256], P('user'), parts along dimension 0, may hold values from 1024 to 4096
- w_mix: bfloat16 [2, 256, 256], replicated, may hold values from -0.375 to 0.375
- w_context: bfloat16 [2, 256, 256], replicated, may hold values from -0.375 to 0.375
- gains: float32 [2, 256], replicated, may hold values from 0.5 to 1.5
- w_up: bfloat16 [2, 256, 1024], replicated, may hold values from -0.375 to 0.375
- w_down: bfloat16 [2, 1024, 256], replicated, may hold values from -0.1875 to 0.1875
Outputs:
- encoded: bfloat16 [256, 4096, 256], P('user', 'tm'), parts along dimension 0
The draws below stay inside these ranges and needn't reach their ends.
There are 8 independent parts, one for each index of `user`. The reference program is written for one: setup_inputs(seed, part) draws one part's arguments, and reference() takes and returns one part's arrays. A program takes and returns all parts, laid end to end along the dimension named above; an argument that names none is the same for every part. Nothing has to cross between parts.
All inputs are finite; a program needn't handle non-finite values.
Results may differ from the reference program's by a relative error of at most 0.012.
Values may be sent and summed in bfloat16 or wider, within the bound.
No kernel may reach another device: no remote copies, remote signals or barrier semaphores. Data moves between devices by JAX's collectives and lax.ppermute only.
A program may use at most 64 MiB of HBM per device.

```python
import jax
import jax.numpy as jnp
from jax import lax

D = 256
FF = 1024
HALF = 32
LAYERS = 2
USERS = 32
NT = 4096


def set_ends(values, stream_key, least, high):
    index_at = [jax.random.randint(jax.random.fold_in(stream_key, axis), (), 0, length) for axis, length in enumerate(values.shape)]
    longest = values.shape.index(max(values.shape))
    beside = index_at[:longest] + [(index_at[longest] + 1) % values.shape[longest]] + index_at[longest + 1:]
    return values.at[tuple(index_at)].set(least).at[tuple(beside)].set(high)


def level_of(stream_key, dims, cuts, smallest, high):
    def one(dim, shards_of):
        heights = jax.random.uniform(jax.random.fold_in(jax.random.fold_in(stream_key, 6), dim), (shards_of,), jnp.float32, smallest / len(cuts), high / len(cuts))
        return jnp.repeat(jnp.exp(heights), dims[dim] // shards_of).reshape((-1,) + (1,) * (len(dims) - dim - 1))

    level = one(*cuts[0])
    for cut in cuts[1:]:
        level = level * one(*cut)
    return level


def gaussian(own_key, dims, spread, limit, split=(), kind=jnp.bfloat16):
    level = level_of(own_key, dims, split, -0.22, 0.18) if split else 1.0
    values = jax.random.normal(own_key, dims, jnp.float32) * spread * level
    return jnp.minimum(jnp.maximum(values, -limit), limit).astype(kind)


def setup_inputs(seed: int = 0, part: int = 0) -> dict:
    streams_of = jax.random.split(jax.random.key(seed), 8)
    part_keys = jax.random.split(jax.random.fold_in(streams_of[7], part), 8)
    events = gaussian(part_keys[0], (USERS, NT, D), 1.0, 6.0, ((1, 64),))
    lengths = set_ends(jax.random.randint(part_keys[1], (USERS,), NT // 4, NT + 1), jax.random.fold_in(part_keys[1], 1), NT // 4, NT).astype(jnp.int32)
    w_mix = gaussian(streams_of[2], (LAYERS, D, D), D ** -0.5, 0.375)
    w_context = gaussian(streams_of[3], (LAYERS, D, D), D ** -0.5, 0.375)
    gains = jnp.clip(1.0 + 0.1 * jax.random.normal(streams_of[4], (LAYERS, D), jnp.float32), 0.5, 1.5)
    w_up = gaussian(streams_of[5], (LAYERS, D, FF), D ** -0.5, 0.375)
    w_down = gaussian(streams_of[6], (LAYERS, FF, D), FF ** -0.5, 0.1875)
    return {"events": events, "lengths": lengths, "w_mix": w_mix, "w_context": w_context, "gains": gains, "w_up": w_up, "w_down": w_down}


def apply_layer(layer_index, current, valid_mask, w_mix, w_context, gains, w_up, w_down):
    as_float = current.astype(jnp.float32)
    seq_len = current.shape[1]
    padded = jnp.pad(as_float, ((0, 0), (HALF, HALF), (0, 0)))
    mixed_rows = jnp.zeros_like(as_float)
    for offset in range(2 * HALF + 1):
        shifted = padded[:, offset:offset + seq_len]
        weight = lax.optimization_barrier(jnp.sum(as_float * shifted, axis=-1)) / D
        weight = lax.optimization_barrier(weight.astype(jnp.bfloat16)).astype(jnp.float32)
        mixed_rows = mixed_rows + weight[..., None] * shifted
    mixed_rows = mixed_rows.astype(jnp.bfloat16)
    position = jnp.arange(seq_len, dtype=jnp.int32).astype(jnp.float32)
    context = (jnp.cumsum(as_float, axis=1) / jnp.sqrt(position + 1.0)[None, :, None]).astype(jnp.bfloat16)
    flat_mix = mixed_rows.reshape(-1, D)
    flat_ctx = context.reshape(-1, D)
    compressed = jnp.dot(flat_mix, w_mix[layer_index], preferred_element_type=jnp.float32)
    compressed = compressed + jnp.dot(flat_ctx, w_context[layer_index], preferred_element_type=jnp.float32)
    summed = as_float.reshape(-1, D) + compressed
    row_mean = lax.optimization_barrier(jnp.mean(summed, axis=-1, keepdims=True))
    row_var = lax.optimization_barrier(jnp.mean((summed - row_mean) ** 2, axis=-1, keepdims=True))
    normed = ((summed - row_mean) / jnp.sqrt(row_var + 1e-05) * gains[layer_index]).astype(jnp.bfloat16)
    hidden = jax.nn.relu(jnp.dot(normed, w_up[layer_index], preferred_element_type=jnp.float32)).astype(jnp.bfloat16)
    result = normed.astype(jnp.float32) + jnp.dot(hidden, w_down[layer_index], preferred_element_type=jnp.float32)
    result = result.reshape(current.shape)
    return jnp.where(valid_mask[..., None], result, 0.0).astype(jnp.bfloat16)

def reference(events, lengths, w_mix, w_context, gains, w_up, w_down):
    position = jnp.arange(events.shape[1], dtype=jnp.int32)
    valid_mask = position[None, :] < lengths[:, None]
    current = jnp.where(valid_mask[..., None], events, jnp.zeros_like(events)).astype(jnp.bfloat16)
    for layer_index in range(LAYERS):
        current = apply_layer(layer_index, current, valid_mask, w_mix, w_context, gains, w_up, w_down)
    return current
```

```python
import functools

import jax
import jax.numpy as jnp
from jax import lax
from jax.experimental import pallas as pl
from jax.experimental.pallas import tpu as pltpu
from jax.sharding import Mesh
from jax.sharding import PartitionSpec as P

D = 256
HALF = 32
LAYERS = 2
TM = ("tm_0", "tm_1", "tm_2")
ROWS = 2 * HALF
WIDE = 2 * ROWS
STEP = 16
PIECE = 4

BF16 = jnp.bfloat16
F32 = jnp.float32
VMEM = pl.BlockSpec(memory_space=pltpu.VMEM)
SMEM = pl.BlockSpec(memory_space=pltpu.SMEM)
ANY = pl.BlockSpec(memory_space=pl.ANY)
HBM = pl.BlockSpec(memory_space=pltpu.HBM)
LIMIT = pltpu.CompilerParams(vmem_limit_bytes=16 << 20)


def in_hbm(x):
    return pltpu.with_memory_space_constraint(x, pltpu.HBM)


def first_position():
    y, z, c = (lax.axis_index(a) for a in TM)
    nz, nc = (lax.axis_size(a) for a in TM[1:])
    return ((y * nz + z) * nc + c) * ROWS


def scale_rows(first_pos):
    t = lax.broadcasted_iota(jnp.int32, (ROWS, D), 0)
    return t, lax.rsqrt((first_pos + t + 1).astype(F32))


def projected(sums, weight):
    coarse = sums.astype(BF16)
    fine = (sums - coarse.astype(F32)).astype(BF16)
    return jnp.dot(coarse, weight, preferred_element_type=F32) + jnp.dot(
        fine, weight, preferred_element_type=F32
    )


def pre_kernel(
    events_ref, lengths_ref, w_ref, head_ref, tail_ref, totals_ref, buf, lens, w, sums, sems, own_sems
):
    users = head_ref.shape[0]
    blocks = sems.shape[0]
    size = users // blocks
    get_lengths = pltpu.make_async_copy(lengths_ref, lens, own_sems.at[0])
    get_w = pltpu.make_async_copy(w_ref.at[0], w, own_sems.at[1])
    get_lengths.start()

    def fetch(i):
        part = pl.ds(i * size, size)
        return pltpu.make_async_copy(events_ref.at[part], buf.at[part], sems.at[i])

    for i in range(blocks):
        fetch(i).start()
    get_w.start()
    first_pos = first_position()
    t = lax.broadcasted_iota(jnp.int32, (ROWS, D), 0)
    get_lengths.wait()
    for i in range(blocks):
        fetch(i).wait()
        rows = []
        for u in range(i * size, (i + 1) * size):
            state = jnp.where(t < lens[u] - first_pos, buf[u].astype(F32), 0.0)
            rows.append(jnp.sum(state, axis=0, keepdims=True))
            state = state.astype(BF16)
            head_ref[u] = state[:HALF]
            tail_ref[u] = state[HALF:]
        sums[i * size : (i + 1) * size] = jnp.concatenate(rows, axis=0)
    get_w.wait()
    totals = projected(sums[...], w[...]).astype(BF16)
    for k in range(totals_ref.shape[0]):
        totals_ref[k] = totals


def pre(events, lengths, w_context, copies):
    users = events.shape[0]
    half = jax.ShapeDtypeStruct((users, HALF, D), BF16)
    return pl.pallas_call(
        pre_kernel,
        in_specs=[HBM, HBM, HBM],
        out_specs=[VMEM, VMEM, VMEM],
        out_shape=[half, half, jax.ShapeDtypeStruct((copies, users, D), BF16)],
        scratch_shapes=[
            pltpu.VMEM(events.shape, BF16),
            pltpu.SMEM(lengths.shape, jnp.int32),
            pltpu.VMEM((D, D), BF16),
            pltpu.VMEM((users, D), F32),
            pltpu.SemaphoreType.DMA((4,)),
            pltpu.SemaphoreType.DMA((2,)),
        ],
        compiler_params=LIMIT,
        cost_estimate=pl.CostEstimate(
            flops=2 * events.size, bytes_accessed=4 * events.size, transcendentals=0
        ),
        name="pre",
    )(events, lengths, w_context)


def mix_kernel(layer, head, tail, low_ref, high_ref, w_mix, w_context, out, *scratch):
    low, high, tri, w, base, sems, side_sems, out_sems = scratch
    users = head.shape[0]
    gets = [
        pltpu.make_async_copy(x.at[layer], w.at[k], sems.at[k])
        for k, x in enumerate((w_mix, w_context))
    ]
    for get in gets:
        get.start()

    def sides(i):
        part = pl.ds(i * STEP, STEP)
        return [
            pltpu.make_async_copy(low_ref.at[part], low.at[part], side_sems.at[2 * i]),
            pltpu.make_async_copy(high_ref.at[part], high.at[part], side_sems.at[2 * i + 1]),
        ]

    for i in range(users // STEP):
        for get in sides(i):
            get.start()
    _, scale = scale_rows(first_position())
    r = lax.broadcasted_iota(jnp.int32, (D, D), 0)
    c = lax.broadcasted_iota(jnp.int32, (D, D), 1)
    tri[...] = jnp.where((c <= r) & (c >= r - lax.rem(r, ROWS)), 1.0, 0.0).astype(BF16)
    r = lax.broadcasted_iota(jnp.int32, (2 * ROWS, 2 * WIDE), 0)
    s = lax.broadcasted_iota(jnp.int32, (2 * ROWS, 2 * WIDE), 1)
    first = r + jnp.where(r >= ROWS, WIDE - ROWS, 0)
    band = (s >= first) & (s <= first + 2 * HALF)
    for get in gets:
        get.wait()

    def store(i):
        part = pl.ds(i * PIECE, PIECE)
        return pltpu.make_async_copy(base.at[part], out.at[part], out_sems.at[i])

    def body(i, carry):
        b = i * STEP
        for get in sides(i):
            get.wait()
        owns, exts, scores = [], [], []
        for u in range(0, STEP, 2):
            u = b + u
            own = [head[u], tail[u], head[u + 1], tail[u + 1]]
            ext = jnp.concatenate(
                [low[u], own[0], own[1], high[u], low[u + 1], own[2], own[3], high[u + 1]], axis=0
            )
            own = jnp.concatenate(own, axis=0)
            owns.append(own)
            exts.append(ext)
            scores.append(
                lax.dot_general(own, ext, (((1,), (1,)), ((), ())), preferred_element_type=F32)
            )
        weights = [jnp.where(band, x * (1.0 / D), 0.0).astype(BF16) for x in scores]
        mixed = [
            jnp.dot(w, e, preferred_element_type=F32).astype(BF16) for w, e in zip(weights, exts)
        ]
        own = jnp.concatenate(owns, axis=0)
        running = [
            jnp.dot(tri[...], own[k : k + D], preferred_element_type=F32).astype(BF16)
            for k in range(0, STEP * ROWS, D)
        ]
        summed = own.astype(F32) + jnp.dot(
            jnp.concatenate(mixed, axis=0), w[0], preferred_element_type=F32
        )
        local = jnp.dot(jnp.concatenate(running, axis=0), w[1], preferred_element_type=F32)
        for k in range(STEP):
            part = slice(k * ROWS, (k + 1) * ROWS)
            base[b + k] = summed[part] + local[part] * scale
            if k % PIECE == PIECE - 1:
                store(i * (STEP // PIECE) + k // PIECE).start()
        return carry

    lax.fori_loop(0, users // STEP, body, 0)
    for i in range(users // PIECE):
        store(i).wait()


def mix(layer, head, tail, low, high, w_mix, w_context):
    users = head.shape[0]
    return pl.pallas_call(
        functools.partial(mix_kernel, layer),
        in_specs=[VMEM] * 2 + [ANY] * 2 + [HBM] * 2,
        out_specs=HBM,
        out_shape=pltpu.HBM((users, ROWS, D), F32),
        scratch_shapes=[
            pltpu.VMEM((users, HALF, D), BF16),
            pltpu.VMEM((users, HALF, D), BF16),
            pltpu.VMEM((D, D), BF16),
            pltpu.VMEM((2, D, D), BF16),
            pltpu.VMEM((users, ROWS, D), F32),
            pltpu.SemaphoreType.DMA((2,)),
            pltpu.SemaphoreType.DMA((2 * (users // STEP),)),
            pltpu.SemaphoreType.DMA((users // PIECE,)),
        ],
        compiler_params=LIMIT,
        cost_estimate=pl.CostEstimate(
            flops=2 * users * ROWS * D * (2 * 2 * WIDE + 3 * D),
            bytes_accessed=8 * users * ROWS * D,
            transcendentals=0,
        ),
        name="mix",
    )(head, tail, low, high, w_mix, w_context)


def post_kernel(layer, last, lengths, base_ref, parts, gains, w_up, w_down, *refs):
    *refs, base, base_sems = refs
    users = base.shape[0]

    def fetch(i):
        part = pl.ds(i * PIECE, PIECE)
        return pltpu.make_async_copy(base_ref.at[part], base.at[part], base_sems.at[i])

    for i in range(users // PIECE):
        fetch(i).start()
    if last:
        out_ref, out_buf, add, sems = refs
    else:
        w_ref, head_ref, tail_ref, totals_ref, add, sums, w, sem = refs
        get_w = pltpu.make_async_copy(w_ref.at[layer + 1], w, sem)
        get_w.start()
    first_pos = first_position()
    t, scale = scale_rows(first_pos)
    add[...] = jnp.sum(parts[...].astype(F32), axis=0)
    gain = gains[layer : layer + 1]

    def store(i):
        part = pl.ds(i * PIECE, PIECE)
        return pltpu.make_async_copy(out_buf.at[part], out_ref.at[part], sems.at[i])

    def body(i, carry):
        b = pl.multiple_of(i * STEP, STEP)
        for k in range(STEP // PIECE):
            fetch(i * (STEP // PIECE) + k).wait()
        more = add[pl.ds(b, STEP)]
        summed = jnp.concatenate(
            [base[b + k] + more[k : k + 1] * scale for k in range(STEP)], axis=0
        )
        mean = jnp.mean(summed, axis=-1, keepdims=True)
        centered = summed - mean
        var = jnp.mean(centered * centered, axis=-1, keepdims=True)
        normed = (centered * lax.rsqrt(var + 1e-05) * gain).astype(BF16)
        hidden = jnp.dot(normed, w_up[layer], preferred_element_type=F32)
        hidden = jnp.maximum(hidden, 0.0).astype(BF16)
        result = normed.astype(F32) + jnp.dot(hidden, w_down[layer], preferred_element_type=F32)
        rows = []
        for k in range(STEP):
            u = b + k
            state = jnp.where(
                t < lengths[u] - first_pos, result[k * ROWS : (k + 1) * ROWS], 0.0
            ).astype(BF16)
            if last:
                out_buf[u] = state
                if k % PIECE == PIECE - 1:
                    store(i * (STEP // PIECE) + k // PIECE).start()
            else:
                head_ref[u] = state[:HALF]
                tail_ref[u] = state[HALF:]
                rows.append(jnp.sum(state.astype(F32), axis=0, keepdims=True))
        if not last:
            sums[pl.ds(b, STEP)] = jnp.concatenate(rows, axis=0)
        return carry

    lax.fori_loop(0, users // STEP, body, 0)
    if last:
        for i in range(users // PIECE):
            store(i).wait()
    else:
        get_w.wait()
        totals = projected(sums[...], w[...]).astype(BF16)
        for k in range(totals_ref.shape[0]):
            totals_ref[k] = totals


def post(layer, last, copies, lengths, base, parts, w_context, gains, w_up, w_down):
    users = base.shape[0]
    in_specs = [SMEM, HBM] + [VMEM] * 4
    args = (lengths, in_hbm(base), parts, gains, w_up, w_down)
    if last:
        out_specs = HBM
        out_shape = jax.ShapeDtypeStruct((users, ROWS, D), BF16)
        scratch = [
            pltpu.VMEM((users, ROWS, D), BF16),
            pltpu.VMEM((users, D), F32),
            pltpu.SemaphoreType.DMA((users // PIECE,)),
        ]
    else:
        half = jax.ShapeDtypeStruct((users, HALF, D), BF16)
        in_specs.append(HBM)
        args += (w_context,)
        out_specs = [VMEM, VMEM, VMEM]
        out_shape = [half, half, jax.ShapeDtypeStruct((copies, users, D), BF16)]
        scratch = [
            pltpu.VMEM((users, D), F32),
            pltpu.VMEM((users, D), F32),
            pltpu.VMEM((D, D), BF16),
            pltpu.SemaphoreType.DMA,
        ]
    scratch += [pltpu.VMEM((users, ROWS, D), F32), pltpu.SemaphoreType.DMA((users // PIECE,))]
    return pl.pallas_call(
        functools.partial(post_kernel, layer, last),
        in_specs=in_specs,
        out_specs=out_specs,
        out_shape=out_shape,
        scratch_shapes=scratch,
        compiler_params=LIMIT,
        cost_estimate=pl.CostEstimate(
            flops=4 * users * ROWS * D * w_up.shape[2],
            bytes_accessed=6 * users * ROWS * D,
            transcendentals=0,
        ),
        name="post",
    )(*args)


def messages(totals):
    y, z, c = (lax.axis_index(a) for a in TM)
    ny, nz, nc = (lax.axis_size(a) for a in TM)
    got = lax.all_to_all(totals, ("tm_0", "tm_2"), 0, 0, tiled=True)
    got = got.reshape(ny, nc, *got.shape[1:]).astype(F32)
    k = jnp.arange(ny)[:, None, None, None]
    j = jnp.arange(nc)[None, :, None, None]
    base = jnp.sum(jnp.where(k < y, got, 0.0), axis=(0, 1))
    row = jnp.sum(jnp.where(k == y, got, 0.0), axis=(0, 1))
    own = jnp.sum(jnp.where((k == y) & (j < c), got, 0.0), axis=(0, 1))
    to = jnp.arange(nz)[:, None, None]
    sent = base[None] + jnp.where(to > z, row[None], jnp.where(to == z, own[None], 0.0))
    return sent.astype(BF16)


def halos(head, tail):
    n = lax.axis_size(TM)
    up = [(i, i + 1) for i in range(n - 1)]
    down = [(i + 1, i) for i in range(n - 1)]
    return lax.ppermute(tail, TM, up), lax.ppermute(head, TM, down)


def per_device(events, lengths, w_mix, w_context, gains, w_up, w_down):
    copies = lax.axis_size(("tm_0", "tm_2"))
    w_mix, w_context = in_hbm(w_mix), in_hbm(w_context)
    head, tail, totals = pre(in_hbm(events), in_hbm(lengths), w_context, copies)
    for layer in range(LAYERS):
        last = layer == LAYERS - 1
        low, high = halos(head, tail)
        parts = lax.all_to_all(messages(totals), "tm_1", 0, 0, tiled=True)
        base = mix(layer, head, tail, low, high, w_mix, w_context)
        out = post(layer, last, copies, lengths, base, parts, w_context, gains, w_up, w_down)
        if last:
            return out
        head, tail, totals = out


def solution(mesh):
    torus = Mesh(
        mesh.devices.reshape(4, 8, 2, mesh.shape["user"]), ("tm_0", "tm_1", "tm_2", "user")
    )
    return jax.shard_map(
        per_device,
        mesh=torus,
        in_specs=(P("user", TM, None), P("user"), P(), P(), P(), P(), P()),
        out_specs=P("user", TM, None),
        check_vma=False,
    )
```

```python
import functools

import jax
import jax.numpy as jnp
from jax import lax
from jax.experimental import pallas as pl
from jax.experimental.pallas import tpu as pltpu
from jax.sharding import Mesh
from jax.sharding import PartitionSpec as P

D = 256
HALF = 32
LAYERS = 2
TM = ("tm_0", "tm_1", "tm_2")
ROWS = 2 * HALF
WIDE = 2 * ROWS
STEP = 16
PIECE = 4

BF16 = jnp.bfloat16
F32 = jnp.float32
VMEM = pl.BlockSpec(memory_space=pltpu.VMEM)
ANY = pl.BlockSpec(memory_space=pl.ANY)
HBM = pl.BlockSpec(memory_space=pltpu.HBM)
LIMIT = pltpu.CompilerParams(vmem_limit_bytes=16 << 20)


def in_hbm(x):
    return pltpu.with_memory_space_constraint(x, pltpu.HBM)


def first_position():
    y, z, c = (lax.axis_index(a) for a in TM)
    nz, nc = (lax.axis_size(a) for a in TM[1:])
    return ((y * nz + z) * nc + c) * ROWS


def place(index, halves):
    half = lax.div(index, HALF)
    back = lax.axis_index(TM[2]) == 1
    return jnp.where(back, halves - 1 - half, half) * HALF + lax.rem(index, HALF)


def half_starts():
    c = lax.axis_index(TM[2])
    return pl.multiple_of(c * HALF, HALF), pl.multiple_of((1 - c) * HALF, HALF)


def scale_rows(first_pos):
    t = place(lax.broadcasted_iota(jnp.int32, (ROWS, D), 0), 2)
    return t, lax.rsqrt((first_pos + t + 1).astype(F32))


def projected(sums, weight):
    coarse = sums.astype(BF16)
    fine = (sums - coarse.astype(F32)).astype(BF16)
    return jnp.dot(coarse, weight, preferred_element_type=F32) + jnp.dot(
        fine, weight, preferred_element_type=F32
    )


def pre_kernel(
    events_ref, lengths_ref, w_ref, outer_ref, inner_ref, totals_ref, buf, lens, w, sums, sems, own_sems
):
    users = outer_ref.shape[0]
    blocks = sems.shape[0]
    size = users // blocks
    get_lengths = pltpu.make_async_copy(lengths_ref, lens, own_sems.at[0])
    get_w = pltpu.make_async_copy(w_ref.at[0], w, own_sems.at[1])
    get_lengths.start()

    def fetch(i):
        part = pl.ds(i * size, size)
        return pltpu.make_async_copy(events_ref.at[part], buf.at[part], sems.at[i])

    for i in range(blocks):
        fetch(i).start()
    get_w.start()
    first_pos = first_position()
    t, _ = scale_rows(first_pos)
    starts = half_starts()
    get_lengths.wait()
    for i in range(blocks):
        fetch(i).wait()
        rows = []
        for u in range(i * size, (i + 1) * size):
            state = jnp.concatenate([buf[u, pl.ds(start, HALF)] for start in starts], axis=0)
            state = jnp.where(t < lens[u] - first_pos, state.astype(F32), 0.0)
            rows.append(jnp.sum(state, axis=0, keepdims=True))
            state = state.astype(BF16)
            outer_ref[u] = state[:HALF]
            inner_ref[u] = state[HALF:]
        sums[i * size : (i + 1) * size] = jnp.concatenate(rows, axis=0)
    get_w.wait()
    totals = projected(sums[...], w[...]).astype(BF16)
    for k in range(totals_ref.shape[0]):
        totals_ref[k] = totals


def pre(events, lengths, w_context, copies):
    users = events.shape[0]
    half = jax.ShapeDtypeStruct((users, HALF, D), BF16)
    return pl.pallas_call(
        pre_kernel,
        in_specs=[HBM, HBM, HBM],
        out_specs=[VMEM, VMEM, VMEM],
        out_shape=[half, half, jax.ShapeDtypeStruct((copies, users, D), BF16)],
        scratch_shapes=[
            pltpu.VMEM(events.shape, BF16),
            pltpu.SMEM(lengths.shape, jnp.int32),
            pltpu.VMEM((D, D), BF16),
            pltpu.VMEM((users, D), F32),
            pltpu.SemaphoreType.DMA((4,)),
            pltpu.SemaphoreType.DMA((2,)),
        ],
        compiler_params=LIMIT,
        cost_estimate=pl.CostEstimate(
            flops=2 * events.size, bytes_accessed=4 * events.size, transcendentals=0
        ),
        name="pre",
    )(events, lengths, w_context)


def mix_kernel(layer, outer, inner, far_ref, near_ref, w_mix, w_context, out, *scratch):
    far, near, tri, w, base, sems, side_sems, out_sems = scratch
    users = outer.shape[0]
    gets = [
        pltpu.make_async_copy(x.at[layer], w.at[k], sems.at[k])
        for k, x in enumerate((w_mix, w_context))
    ]
    for get in gets:
        get.start()

    def sides(i):
        part = pl.ds(i * STEP, STEP)
        return [
            pltpu.make_async_copy(far_ref.at[part], far.at[part], side_sems.at[2 * i]),
            pltpu.make_async_copy(near_ref.at[part], near.at[part], side_sems.at[2 * i + 1]),
        ]

    for i in range(users // STEP):
        for get in sides(i):
            get.start()
    _, scale = scale_rows(first_position())
    r = lax.broadcasted_iota(jnp.int32, (D, D), 0)
    c = lax.broadcasted_iota(jnp.int32, (D, D), 1)
    same = lax.div(r, ROWS) == lax.div(c, ROWS)
    earlier = place(lax.rem(c, ROWS), 2) <= place(lax.rem(r, ROWS), 2)
    tri[...] = jnp.where(same & earlier, 1.0, 0.0).astype(BF16)
    r = lax.broadcasted_iota(jnp.int32, (2 * ROWS, 2 * WIDE), 0)
    s = lax.broadcasted_iota(jnp.int32, (2 * ROWS, 2 * WIDE), 1)
    apart = place(lax.rem(s, WIDE), 4) - place(lax.rem(r, ROWS), 2)
    band = (lax.div(r, ROWS) == lax.div(s, WIDE)) & (apart >= 0) & (apart <= 2 * HALF)
    for get in gets:
        get.wait()

    def store(i):
        part = pl.ds(i * PIECE, PIECE)
        return pltpu.make_async_copy(base.at[part], out.at[part], out_sems.at[i])

    def body(i, carry):
        b = i * STEP
        for get in sides(i):
            get.wait()
        owns, exts, scores = [], [], []
        for u in range(0, STEP, 2):
            u = b + u
            own = [outer[u], inner[u], outer[u + 1], inner[u + 1]]
            ext = jnp.concatenate(
                [far[u], own[0], own[1], near[u], far[u + 1], own[2], own[3], near[u + 1]], axis=0
            )
            own = jnp.concatenate(own, axis=0)
            owns.append(own)
            exts.append(ext)
            scores.append(
                lax.dot_general(own, ext, (((1,), (1,)), ((), ())), preferred_element_type=F32)
            )
        weights = [jnp.where(band, x * (1.0 / D), 0.0).astype(BF16) for x in scores]
        mixed = [
            jnp.dot(w, e, preferred_element_type=F32).astype(BF16) for w, e in zip(weights, exts)
        ]
        own = jnp.concatenate(owns, axis=0)
        running = [
            jnp.dot(tri[...], own[k : k + D], preferred_element_type=F32).astype(BF16)
            for k in range(0, STEP * ROWS, D)
        ]
        summed = own.astype(F32) + jnp.dot(
            jnp.concatenate(mixed, axis=0), w[0], preferred_element_type=F32
        )
        local = jnp.dot(jnp.concatenate(running, axis=0), w[1], preferred_element_type=F32)
        for k in range(STEP):
            part = slice(k * ROWS, (k + 1) * ROWS)
            base[b + k] = summed[part] + local[part] * scale
            if k % PIECE == PIECE - 1:
                store(i * (STEP // PIECE) + k // PIECE).start()
        return carry

    lax.fori_loop(0, users // STEP, body, 0)
    for i in range(users // PIECE):
        store(i).wait()


def mix(layer, outer, inner, far, near, w_mix, w_context):
    users = outer.shape[0]
    return pl.pallas_call(
        functools.partial(mix_kernel, layer),
        in_specs=[VMEM] * 2 + [ANY] * 2 + [HBM] * 2,
        out_specs=HBM,
        out_shape=pltpu.HBM((users, ROWS, D), F32),
        scratch_shapes=[
            pltpu.VMEM((users, HALF, D), BF16),
            pltpu.VMEM((users, HALF, D), BF16),
            pltpu.VMEM((D, D), BF16),
            pltpu.VMEM((2, D, D), BF16),
            pltpu.VMEM((users, ROWS, D), F32),
            pltpu.SemaphoreType.DMA((2,)),
            pltpu.SemaphoreType.DMA((2 * (users // STEP),)),
            pltpu.SemaphoreType.DMA((users // PIECE,)),
        ],
        compiler_params=LIMIT,
        cost_estimate=pl.CostEstimate(
            flops=2 * users * ROWS * D * (2 * 2 * WIDE + 3 * D),
            bytes_accessed=8 * users * ROWS * D,
            transcendentals=0,
        ),
        name="mix",
    )(outer, inner, far, near, w_mix, w_context)


def post_kernel(layer, last, lengths_ref, base_ref, parts, gains, w_up, w_down, *refs):
    *refs, base, base_sems, lengths, lengths_sem = refs
    users = base.shape[0]
    get_lengths = pltpu.make_async_copy(lengths_ref, lengths, lengths_sem)

    def fetch(i):
        part = pl.ds(i * PIECE, PIECE)
        return pltpu.make_async_copy(base_ref.at[part], base.at[part], base_sems.at[i])

    for i in range(STEP // PIECE):
        fetch(i).start()
    get_lengths.start()
    for i in range(STEP // PIECE, users // PIECE):
        fetch(i).start()
    if last:
        out_ref, out_buf, add, sems = refs
    else:
        w_ref, outer_ref, inner_ref, totals_ref, add, sums, w, sem = refs
        get_w = pltpu.make_async_copy(w_ref.at[layer + 1], w, sem)
        get_w.start()
    first_pos = first_position()
    t, scale = scale_rows(first_pos)
    add[...] = jnp.sum(parts[...].astype(F32), axis=0)
    gain = gains[layer : layer + 1]
    starts = half_starts()
    get_lengths.wait()

    def store(i):
        part = pl.ds(i * PIECE, PIECE)
        return pltpu.make_async_copy(out_buf.at[part], out_ref.at[part], sems.at[i])

    def body(i, carry):
        b = pl.multiple_of(i * STEP, STEP)
        for k in range(STEP // PIECE):
            fetch(i * (STEP // PIECE) + k).wait()
        more = add[pl.ds(b, STEP)]
        summed = jnp.concatenate(
            [base[b + k] + more[k : k + 1] * scale for k in range(STEP)], axis=0
        )
        mean = jnp.mean(summed, axis=-1, keepdims=True)
        centered = summed - mean
        var = jnp.mean(centered * centered, axis=-1, keepdims=True)
        normed = (centered * lax.rsqrt(var + 1e-05) * gain).astype(BF16)
        hidden = jnp.dot(normed, w_up[layer], preferred_element_type=F32)
        hidden = jnp.maximum(hidden, 0.0).astype(BF16)
        result = normed.astype(F32) + jnp.dot(hidden, w_down[layer], preferred_element_type=F32)
        rows = []
        for k in range(STEP):
            u = b + k
            state = jnp.where(
                t < lengths[u] - first_pos, result[k * ROWS : (k + 1) * ROWS], 0.0
            ).astype(BF16)
            if last:
                out_buf[u, pl.ds(starts[0], HALF)] = state[:HALF]
                out_buf[u, pl.ds(starts[1], HALF)] = state[HALF:]
                if k % PIECE == PIECE - 1:
                    store(i * (STEP // PIECE) + k // PIECE).start()
            else:
                outer_ref[u] = state[:HALF]
                inner_ref[u] = state[HALF:]
                rows.append(jnp.sum(state.astype(F32), axis=0, keepdims=True))
        if not last:
            sums[pl.ds(b, STEP)] = jnp.concatenate(rows, axis=0)
        return carry

    lax.fori_loop(0, users // STEP, body, 0)
    if last:
        for i in range(users // PIECE):
            store(i).wait()
    else:
        get_w.wait()
        totals = projected(sums[...], w[...]).astype(BF16)
        for k in range(totals_ref.shape[0]):
            totals_ref[k] = totals


def post(layer, last, copies, lengths, base, parts, w_context, gains, w_up, w_down):
    users = base.shape[0]
    in_specs = [HBM, HBM] + [VMEM] * 4
    args = (in_hbm(lengths), in_hbm(base), parts, gains, w_up, w_down)
    if last:
        out_specs = HBM
        out_shape = jax.ShapeDtypeStruct((users, ROWS, D), BF16)
        scratch = [
            pltpu.VMEM((users, ROWS, D), BF16),
            pltpu.VMEM((users, D), F32),
            pltpu.SemaphoreType.DMA((users // PIECE,)),
        ]
    else:
        half = jax.ShapeDtypeStruct((users, HALF, D), BF16)
        in_specs.append(HBM)
        args += (w_context,)
        out_specs = [VMEM, VMEM, VMEM]
        out_shape = [half, half, jax.ShapeDtypeStruct((copies, users, D), BF16)]
        scratch = [
            pltpu.VMEM((users, D), F32),
            pltpu.VMEM((users, D), F32),
            pltpu.VMEM((D, D), BF16),
            pltpu.SemaphoreType.DMA,
        ]
    scratch += [
        pltpu.VMEM((users, ROWS, D), F32),
        pltpu.SemaphoreType.DMA((users // PIECE,)),
        pltpu.SMEM(lengths.shape, jnp.int32),
        pltpu.SemaphoreType.DMA,
    ]
    return pl.pallas_call(
        functools.partial(post_kernel, layer, last),
        in_specs=in_specs,
        out_specs=out_specs,
        out_shape=out_shape,
        scratch_shapes=scratch,
        compiler_params=LIMIT,
        cost_estimate=pl.CostEstimate(
            flops=4 * users * ROWS * D * w_up.shape[2],
            bytes_accessed=6 * users * ROWS * D,
            transcendentals=0,
        ),
        name="post",
    )(*args)


def messages(totals):
    y, z, c = (lax.axis_index(a) for a in TM)
    ny, nz, nc = (lax.axis_size(a) for a in TM)
    got = lax.all_to_all(totals, ("tm_0", "tm_2"), 0, 0, tiled=True)
    got = got.reshape(ny, nc, *got.shape[1:]).astype(F32)
    k = jnp.arange(ny)[:, None, None, None]
    j = jnp.arange(nc)[None, :, None, None]
    base = jnp.sum(jnp.where(k < y, got, 0.0), axis=(0, 1))
    row = jnp.sum(jnp.where(k == y, got, 0.0), axis=(0, 1))
    own = jnp.sum(jnp.where((k == y) & (j < c), got, 0.0), axis=(0, 1))
    to = jnp.arange(nz)[:, None, None]
    sent = base[None] + jnp.where(to > z, row[None], jnp.where(to == z, own[None], 0.0))
    return sent.astype(BF16)


def halos(outer, inner):
    n = lax.axis_size(TM)

    def swapped(first):
        pairs = [(i, i + 1) for i in range(first, n - 1, 2)]
        return pairs + [(j, i) for i, j in pairs]

    return lax.ppermute(outer, TM, swapped(1)), lax.ppermute(inner, TM, swapped(0))


def per_device(events, lengths, w_mix, w_context, gains, w_up, w_down):
    copies = lax.axis_size(("tm_0", "tm_2"))
    w_mix, w_context = in_hbm(w_mix), in_hbm(w_context)
    outer, inner, totals = pre(in_hbm(events), in_hbm(lengths), w_context, copies)
    for layer in range(LAYERS):
        last = layer == LAYERS - 1
        far, near = halos(outer, inner)
        parts = lax.all_to_all(messages(totals), "tm_1", 0, 0, tiled=True)
        base = mix(layer, outer, inner, far, near, w_mix, w_context)
        out = post(layer, last, copies, lengths, base, parts, w_context, gains, w_up, w_down)
        if last:
            return out
        outer, inner, totals = out


def solution(mesh):
    torus = Mesh(
        mesh.devices.reshape(4, 8, 2, mesh.shape["user"]), ("tm_0", "tm_1", "tm_2", "user")
    )
    return jax.shard_map(
        per_device,
        mesh=torus,
        in_specs=(P("user", TM, None), P("user"), P(), P(), P(), P(), P()),
        out_specs=P("user", TM, None),
        check_vma=False,
    )
```
